512 devices in a mesh: tm: 8 (over y_hi, core), space: 64 (over y_lo, z, x).
Axes of the slice: x: 4, y: 8 (y_hi: 4, y_lo: 2; y = y_hi * 2 + y_lo), z: 8, core: 2. Of those that a mesh axis runs over, the one named last changes fastest.
Arguments:
- start_states: float32 [8, 3, 512, 4096], P('tm', None, 'space'), may hold values from -6 to 6
- coarse_gain: float32 [3, 512, 4096], P(None, 'space'), may hold values from 0.55 to 0.95
- depth_level: int32 [512, 4096], P('space'), may hold values from 0 to 63
- depth_table: float32 [64], replicated, may hold values from 0.2 to 1
- wet: int32 [512, 4096], P('space'), may hold values 0 or 1
- block_count: int32 [64], P('space'), may hold values from 1 to 8, 320 in all
- neighbour: int32 [512, 4], P('space'), may hold values from -1 to 7
- coriolis: float32 [512, 4096], P('space'), may hold values from -0.5 to 0.5
- tide: float32 [2, 512, 4096], P(None, 'space'), may hold values from -2 to 2
Outputs:
- new_states: float32 [8, 3, 512, 4096], P('tm', None, 'space')
The draws below stay inside these ranges and needn't reach their ends.
Inputs may be any that keep to these rules, and one draw needn't show every extreme that they name: `block_count`: each column's count is the number of its first slots that hold ocean blocks; some column holds 8. `neighbour`: entries 0 and 1 name slots of the same column, entries 2 and 3 slots of the next and the previous column along the periodic longitude; -1 is a closed face.
All inputs are finite; a program needn't handle non-finite values. No bound on the sum of `wet` on one device may be relied on, other than what follows from the above.
Results may differ from the reference program's by a relative error of at most 0.00007.
Values sent between devices are 32-bit elements; how exact they have to be, the bound alone decides.
A program may use at most 64 MiB of HBM per device.

```python
import math
import jax
import jax.numpy as jnp
import numpy as np

BS = 64
CELLS = 4096
NB = 8
STEPS = 6
LEVELS = 64
SLICES = 8
SLOTS = 512
N_SPACE = 64


def with_ends(values, stream_key, least, top_value):
    shape = values.shape
    index_at = [jax.random.randint(jax.random.fold_in(stream_key, axis), (), 0, shape[axis]) for axis in range(len(shape))]
    values = values.at[tuple(index_at)].set(least)
    longest = shape.index(max(shape))
    index_at[longest] = (index_at[longest] + 1) % shape[longest]
    return values.at[tuple(index_at)].set(top_value)


def steps_of(rng, dims, cuts, least, high):
    gain = 1.0
    for position, shards_of in cuts:
        heights = jax.random.uniform(jax.random.fold_in(jax.random.fold_in(rng, 6), position), (shards_of,), jnp.float32, least / len(cuts), high / len(cuts))
        gain = gain * jnp.repeat(jnp.exp(heights), dims[position] // shards_of).reshape((-1,) + (1,) * (len(dims) - 1 - position))
    return gain


def length_profile(amount, total, limit, lean):
    loads = [(1 << 20) // math.isqrt(rank ** lean) + 1 for rank in range(2, amount + 1)]
    surplus, counts = total - limit - (amount - 1), [1] * (amount - 1)
    while surplus > 0:
        candidates = [i for i in range(amount - 1) if counts[i] < limit]
        whole, budget = sum([loads[i] for i in candidates]), surplus
        for i in candidates:
            extra = min(limit - counts[i], max(1, budget * loads[i] // whole), surplus)
            counts[i] = counts[i] + extra
            surplus = surplus - extra
    return np.array([limit] + counts)


def uneven_parts(key, count, total, limit, slope):
    if count == 2:
        one = jax.random.randint(key, (), max(1, total - limit), min(limit, total - 1) + 1)
        return jnp.stack([one, total - one])
    tallies = jnp.asarray(length_profile(count, total, limit, slope), jnp.int32)
    pairs = (count - 1) // 2
    source_of, taker = tallies[1:1 + 2 * pairs:2], tallies[2:2 + 2 * pairs:2]
    margin = jnp.minimum(source_of - 1, limit - taker)
    shifted = jax.random.randint(jax.random.fold_in(key, 1), (pairs,), 0, 1 << 20) % (margin + 1)
    tallies = tallies.at[1:1 + 2 * pairs:2].set(source_of - shifted).at[2:2 + 2 * pairs:2].set(taker + shifted)
    return tallies[jax.random.permutation(jax.random.fold_in(key, 2), count)]


def scatter_about(own_key, dims, spread, limit, shards=(), kind=jnp.bfloat16):
    values = jax.random.normal(own_key, dims, jnp.float32) * spread
    if len(shards) > 0:
        values = steps_of(own_key, dims, shards, -0.22, 0.18) * values
    return jnp.clip(values, min=-limit, max=limit).astype(kind)


def setup_inputs(seed: int = 0) -> dict:
    key_of = jax.random.split(jax.random.key(seed), 10)
    return {
        "start_states": scatter_about(key_of[0], (SLICES, 3, SLOTS, CELLS), 1.0, 6.0, ((0, 8), (2, 64)), jnp.float32),
        "coarse_gain": jnp.clip(jnp.exp(math.log(0.95) - 0.54654367 * jax.random.uniform(key_of[1], (3, SLOTS, CELLS), jnp.float32) ** steps_of(key_of[1], (3, SLOTS, CELLS), ((1, 64),), -0.2, 0.2)), 0.55, 0.95),
        "depth_level": with_ends(jax.random.randint(key_of[2], (SLOTS, CELLS), 0, LEVELS), jax.random.fold_in(key_of[2], 1), 0, LEVELS - 1).astype(jnp.int32),
        "depth_table": jnp.clip(jnp.exp(jax.random.uniform(key_of[3], (LEVELS,), jnp.float32, math.log(0.2), math.log(1.0))), 0.2, 1.0),
        "wet": with_ends((jax.random.randint(key_of[4], (SLOTS, CELLS), 0, 8) < 7).astype(jnp.int32), jax.random.fold_in(key_of[4], 1), 0, 1),
        "block_count": uneven_parts(key_of[5], N_SPACE, N_SPACE * NB * 5 // 8, NB, 1).astype(jnp.int32),
        "neighbour": with_ends(jax.random.randint(key_of[6], (SLOTS, 4), -1, NB), jax.random.fold_in(key_of[6], 1), -1, NB - 1).astype(jnp.int32),
        "coriolis": jnp.clip(jax.random.uniform(key_of[7], (SLOTS, CELLS), jnp.float32, -0.5, 0.5) * steps_of(key_of[7], (SLOTS, CELLS), ((0, 64),), -0.4, 0.0), -0.5, 0.5),
        "tide": scatter_about(key_of[8], (2, SLOTS, CELLS), 0.3, 2.0, ((1, 64),), jnp.float32),
    }


def take_edges(edges, index):
    valid = (index >= 0).astype(edges.dtype)
    return jnp.take(edges, jnp.maximum(index, 0).astype(jnp.int32), axis=0) * valid[:, None]


def across(field, west_ghost, east_ghost):
    column = jnp.arange(field.shape[-1]) % BS
    zero = jnp.zeros(field.shape[:-1] + (1,), field.dtype)
    east = jnp.where(column == BS - 1, jnp.repeat(east_ghost, BS, axis=-1), jnp.concatenate([field[:, 1:], zero], -1))
    west = jnp.where(column == 0, jnp.repeat(west_ghost, BS, axis=-1), jnp.concatenate([zero, field[:, :-1]], -1))
    return 0.5 * (east - west)


def along(field, north_ghost, south_ghost):
    north = jnp.concatenate([field[:, BS:], north_ghost], -1)
    south = jnp.concatenate([south_ghost, field[:, :-BS]], -1)
    return 0.5 * (north - south)


def reference(start_states, coarse_gain, depth_level, depth_table, wet, block_count, neighbour, coriolis, tide):
    slot = jnp.arange(SLOTS).astype(jnp.int32)
    column = slot // NB
    count = jnp.repeat(block_count, NB)
    live = wet.astype(jnp.float32) * ((slot % NB) < count).astype(jnp.float32)[:, None]
    depth = jnp.take(depth_table, depth_level)

    def global_id(entry, col):
        return jnp.where(entry >= 0, col * NB + entry, -1).astype(jnp.int32)

    north_id = global_id(neighbour[:, 0], column)
    south_id = global_id(neighbour[:, 1], column)
    east_id = global_id(neighbour[:, 2], (column + 1) % N_SPACE)
    west_id = global_id(neighbour[:, 3], (column + N_SPACE - 1) % N_SPACE)

    def grad_x(field):
        return across(field, take_edges(field[:, BS - 1::BS], west_id), take_edges(field[:, 0::BS], east_id))

    def grad_y(field):
        return along(field, take_edges(field[:, :BS], north_id), take_edges(field[:, -BS:], south_id))

    start = start_states * live
    omega = 2.0 * math.pi / (SLICES * STEPS)
    fine = []
    for index in range(SLICES):
        level, east_vel, north_vel = start[index, 0], start[index, 1], start[index, 2]
        for step in range(STEPS):
            angle = jnp.float32((index * STEPS + step) * omega)
            source = tide[0] * jnp.cos(angle) + tide[1] * jnp.sin(angle)
            div = grad_x(depth * east_vel) + grad_y(depth * north_vel)
            level = (level + 0.3 * (source - div)) * live
            new_east = (east_vel + 0.3 * (coriolis * north_vel - grad_x(level) - 0.05 * east_vel)) * live
            north_vel = (north_vel + 0.3 * (-coriolis * east_vel - grad_y(level) - 0.05 * north_vel)) * live
            east_vel = new_east
        fine.append(jnp.stack([level, east_vel, north_vel]))
    defect = jnp.stack(fine) - coarse_gain * start
    total = jnp.zeros_like(defect)
    for lag in range(1, SLICES + 1):
        total = total + coarse_gain ** (lag - 1) * jnp.roll(defect, lag, axis=0)
    return total / (1.0 - coarse_gain ** SLICES)
```

```python
import functools
import math

import jax
import jax.numpy as jnp
import numpy as np
from jax import lax
from jax.experimental import pallas as pl
from jax.experimental.pallas import tpu as pltpu
from jax.sharding import PartitionSpec as P

BS = 64
STEPS = 6
SLICES = 8
NV = 32
CHUNK = 16
HALF = 48
PART = 12
MESH = pl.DeviceIdType.MESH


def lanes():
    return lax.broadcasted_iota(jnp.int32, (8, 128), 1)


def turn(x, by):
    return pltpu.roll(x, by % 128, axis=x.ndim - 1)


def permuted(x, index, valid):
    if x.ndim == 2:
        picked = jnp.take_along_axis(x, index, axis=0, mode="promise_in_bounds")
        return jnp.where(valid, picked, 0.0)
    return jnp.stack([permuted(x[i], index, valid) for i in range(x.shape[0])])


def kernel(
    n_space,
    start_hbm, gain_hbm, level_hbm, wet_hbm, cor_hbm, tide_hbm, table_ref, nb_ref, count_ref, trig_ref,
    out_ref,
    start, gain, lev, wet, cor, tide, table,
    depth_o, mask_o, t0_o, t1_o, c_o, eta_o, u_o, v_o, ry_o,
    depth_s, mask_s, t0_s, t1_s, c_s, eta_s, u_s, v_s, ry_s,
    pack_r, pack_l, got_r, got_l, nb_r, nb_l, nbgot_r, nbgot_l,
    eo, swap, cpart, cgot, xown, xgot, xsend, final,
    load_sem, hs_r, hr_r, hs_l, hr_l, nsem, chip_sem, cs, cr, xs, xr, fs, fr,
):
    m = lax.axis_index("tm")
    c = lax.axis_index("space")
    core = lax.rem(m, 2)
    chip = lax.div(m, 2)
    right = (m, lax.rem(c + 1, n_space))
    left = (m, lax.rem(c + n_space - 1, n_space))
    twin = (m + 1 - 2 * core, c)

    def chip_at(d):
        return (lax.rem(chip + d, 4) * 2 + core, c)

    barrier = pltpu.get_barrier_semaphore()
    peers = [right, left, twin, chip_at(1), chip_at(2), chip_at(3)]
    for peer in peers:
        pl.semaphore_signal(barrier, inc=1, device_id=peer, device_id_type=MESH)

    loads = []
    for j, (src, dst) in enumerate(
        [(wet_hbm, wet), (level_hbm, lev), (start_hbm, start), (cor_hbm, cor), (tide_hbm, tide), (gain_hbm, gain)]
    ):
        copy = pltpu.make_async_copy(src, dst, load_sem.at[j])
        copy.start()
        loads.append(copy)

    lane = lanes()
    low = lane < 64
    col = lane & 63
    group = (lane >> 4) & 3
    near = col < 32

    table[...] = jnp.zeros_like(table)
    table[:, 0:64] = jnp.broadcast_to(table_ref[...], (8, 64))
    nb = nb_ref[...]
    n_own, s_own, e_own, w_own = [jnp.broadcast_to(nb[:, j : j + 1], (8, 128)) for j in range(4)]
    for j, (to_right, to_left) in enumerate([(n_own, n_own), (s_own, s_own), (e_own, w_own)]):
        nb_r[j] = to_right
        nb_l[j] = to_left
    slot_live = lax.broadcasted_iota(jnp.int32, (8, 128), 0) < count_ref[0]

    def packed(value, into, k0):
        for q in range(value.shape[0] // 4):
            to_r = to_l = value[4 * q]
            for i in range(1, 4):
                turned = turn(value[4 * q + i], 16 * i)
                to_r = jnp.where(group == (i + 3) % 4, turned, to_r)
                to_l = jnp.where(group == i, turned, to_l)
            pack_r[into, k0 // 4 + q] = to_r
            pack_l[into, k0 // 4 + q] = to_l

    def halo(j):
        return (
            pltpu.make_async_remote_copy(
                pack_r.at[j], got_r.at[j], hs_r.at[j], hr_r.at[j], device_id=right, device_id_type=MESH
            ),
            pltpu.make_async_remote_copy(
                pack_l.at[j], got_l.at[j], hs_l.at[j], hr_l.at[j], device_id=left, device_id_type=MESH
            ),
        )

    n_copies = (
        pltpu.make_async_remote_copy(nb_r, nbgot_r, nsem.at[0], nsem.at[1], device_id=right, device_id_type=MESH),
        pltpu.make_async_remote_copy(nb_l, nbgot_l, nsem.at[2], nsem.at[3], device_id=left, device_id_type=MESH),
    )
    halos = [halo(j) for j in range(8)]
    chunks = range(0, NV, CHUNK)

    loads[0].wait()
    for k0 in chunks:
        ks = pl.ds(k0, CHUNK)
        live = jnp.where(jnp.logical_and(wet[ks] != 0, slot_live[None]), 0.15, 0.0)
        mask_o[ks] = live
        packed(live, 0, k0)
    loads[1].wait()
    entries = table[...]
    for k0 in chunks:
        ks = pl.ds(k0, CHUNK)
        index = lev[ks]
        depth = jnp.stack(
            [jnp.take_along_axis(entries, index[i], axis=1, mode="promise_in_bounds") for i in range(CHUNK)]
        )
        depth_o[ks] = depth
        packed(depth, 1, k0)
    pl.semaphore_wait(barrier, len(peers))
    for copy in n_copies:
        copy.start()
    for j in (0, 1):
        for copy in halos[j]:
            copy.start()
    loads[2].wait()
    for j, (field, state) in enumerate(((1, u_o), (2, v_o), (0, eta_o))):
        for k0 in chunks:
            ks = pl.ds(k0, CHUNK)
            value = jnp.where(mask_o[ks] > 0.0, start[field, ks], 0.0)
            start[field, ks] = value
            state[ks] = value
            packed(value, 2 + j, k0)
        for copy in halos[2 + j]:
            copy.start()
    loads[4].wait()
    for j, into in enumerate((t0_o, t1_o)):
        for k0 in chunks:
            ks = pl.ds(k0, CHUNK)
            value = (2.0 * mask_o[ks]) * tide[j, ks]
            into[ks] = value
            packed(value, 5 + j, k0)
        for copy in halos[5 + j]:
            copy.start()
    loads[3].wait()
    for k0 in chunks:
        ks = pl.ds(k0, CHUNK)
        value = 0.3 * cor[ks]
        c_o[ks] = value
        packed(value, 7, k0)
    for copy in halos[7]:
        copy.start()
    loads[5].wait()

    for copy in n_copies:
        copy.wait_recv()
    n_r, s_r, w_r = nbgot_l[0], nbgot_l[1], nbgot_l[2]
    n_l, s_l, e_l = nbgot_r[0], nbgot_r[1], nbgot_r[2]

    def lookup(index):
        return jnp.maximum(index, 0), index >= 0

    x_own = lookup(jnp.where(near, e_own, w_own))
    y_own = lookup(jnp.where(low, s_own, n_own))
    x_strip = lookup(jnp.where(near, e_l, w_r))
    y_strip = lookup(jnp.where(low, jnp.where(near, n_r, n_l), jnp.where(near, s_r, s_l)))

    for j, into in enumerate((mask_s, depth_s, u_s, v_s, eta_s, t0_s, t1_s, c_s)):
        for copy in halos[j]:
            copy.wait_recv()
        for q in range(NV // 4):
            from_l, from_r = got_r[j, q], got_l[j, q]
            for i in range(4):
                both = jnp.where(group == i, from_r, from_l)
                into[4 * q + i] = turn(both, 64 - 16 * i)

    first = col == 0
    last = col == 63

    def slope_x(own, strip):
        strip_at = permuted(strip, *x_own)
        own_at = permuted(own, *x_strip)
        d_own = turn(jnp.where(first, strip_at, own), -1) - turn(jnp.where(last, strip_at, own), 1)
        d_strip = turn(jnp.where(first, own_at, strip), -1) - turn(jnp.where(last, own_at, strip), 1)
        return d_own, d_strip

    def slope_y_own(k0):
        before, here, after = ry_o[pl.ds(k0, CHUNK)], ry_o[pl.ds(k0 + 1, CHUNK)], ry_o[pl.ds(k0 + 2, CHUNK)]
        return jnp.where(low, here, after) - jnp.where(low, before, here)

    def slope_y_strip(k0):
        before, here, after = ry_s[pl.ds(k0, CHUNK)], ry_s[pl.ds(k0 + 1, CHUNK)], ry_s[pl.ds(k0 + 2, CHUNK)]
        return jnp.where(low, after, here) - jnp.where(low, here, before)

    def ends(strip):
        ends_own = permuted(jnp.where(low, ry_o[NV], ry_o[1]), *y_own)
        ry_o[0] = ends_own
        ry_o[NV + 1] = ends_own
        if strip:
            ends_strip = permuted(jnp.where(low, ry_s[1], ry_s[NV]), *y_strip)
            ry_s[0] = ends_strip
            ry_s[NV + 1] = ends_strip

    for k0 in chunks:
        ks, up = pl.ds(k0, CHUNK), pl.ds(k0 + 1, CHUNK)
        ry_o[up] = turn(depth_o[ks] * v_o[ks], 64)
        ry_s[up] = turn(depth_s[ks] * v_s[ks], 64)
    ends(True)

    def surface(step):
        cosine = trig_ref[m * STEPS + step]
        sine = trig_ref[SLICES * STEPS + m * STEPS + step]
        keep = []
        for k0 in chunks:
            ks = pl.ds(k0, CHUNK)
            dx_o, dx_s = slope_x(depth_o[ks] * u_o[ks], depth_s[ks] * u_s[ks])
            for eta, mask, t0, t1, dx, dy in (
                (eta_o, mask_o, t0_o, t1_o, dx_o, slope_y_own(k0)),
                (eta_s, mask_s, t0_s, t1_s, dx_s, slope_y_strip(k0)),
            ):
                eta[ks] = eta[ks] + (t0[ks] * cosine + t1[ks] * sine) - mask[ks] * (dx + dy)
        for k0 in chunks:
            ks, up = pl.ds(k0, CHUNK), pl.ds(k0 + 1, CHUNK)
            ry_o[up] = turn(eta_o[ks], 64)
            ry_s[up] = turn(eta_s[ks], 64)
        ends(True)

    def one_step(step, carry):
        surface(step)
        for k0 in chunks:
            ks = pl.ds(k0, CHUNK)
            dx_o, dx_s = slope_x(eta_o[ks], eta_s[ks])
            for u_ref, v_ref, mask, cc, dx, dy in (
                (u_o, v_o, mask_o, c_o, dx_o, slope_y_own(k0)),
                (u_s, v_s, mask_s, c_s, dx_s, slope_y_strip(k0)),
            ):
                u, v = u_ref[ks], v_ref[ks]
                u_ref[ks] = 0.985 * u + cc[ks] * jnp.where(mask[ks] > 0.0, v, 0.0) - mask[ks] * dx
                v_ref[ks] = 0.985 * v - cc[ks] * jnp.where(mask[ks] > 0.0, u, 0.0) - mask[ks] * dy
        for k0 in chunks:
            ks, up = pl.ds(k0, CHUNK), pl.ds(k0 + 1, CHUNK)
            ry_o[up] = turn(depth_o[ks] * v_o[ks], 64)
            ry_s[up] = turn(depth_s[ks] * v_s[ks], 64)
        ends(True)
        return carry

    lax.fori_loop(0, STEPS - 1, one_step, 0)
    surface(STEPS - 1)

    def defect(field, ks, fine):
        return fine - gain[field, ks] * start[field, ks]

    for k0 in chunks:
        ks = pl.ds(k0, CHUNK)
        final[0, pl.ds(k0, CHUNK)] = defect(0, ks, eta_o[ks])
        dx, _ = slope_x(eta_o[ks], eta_s[ks])
        dy = slope_y_own(k0)
        u, v = u_o[ks], v_o[ks]
        new_u = 0.985 * u + c_o[ks] * v - mask_o[ks] * dx
        new_v = 0.985 * v - c_o[ks] * u - mask_o[ks] * dy
        half, at = divmod(NV + k0, HALF)
        final[half, pl.ds(at, CHUNK)] = defect(1, ks, new_u)
        final[1, pl.ds(16 + k0, CHUNK)] = defect(2, ks, new_v)

    swap_copy = pltpu.make_async_remote_copy(
        final.at[1 - core], eo.at[core], chip_sem.at[0], chip_sem.at[1], device_id=twin, device_id_type=MESH
    )
    swap_copy.start()
    eo[core] = final[core]
    swap_copy.wait_recv()

    def gain_of(p):
        return swap[pl.ds(p * PART, PART)]

    @pl.when(core == 0)
    def _():
        swap[pl.ds(0, NV)] = gain[0]
        swap[pl.ds(NV, 16)] = gain[1, 0:16]

    @pl.when(core == 1)
    def _():
        swap[pl.ds(0, 16)] = gain[1, 16:32]
        swap[pl.ds(16, NV)] = gain[2]

    c_copies = {}
    for d in (2, 1, 3, 0):
        p = lax.rem(chip + d, 4)
        ps = pl.ds(p * PART, PART)
        cpart[d] = eo[1, ps] + gain_of(p) * eo[0, ps]
        if d:
            c_copies[d] = pltpu.make_async_remote_copy(
                cpart.at[d], cgot.at[d], cs.at[d], cr.at[d], device_id=chip_at(d), device_id_type=MESH
            )
            c_copies[d].start()

    g = gain_of(chip)
    g2 = g * g
    g4 = g2 * g2
    inverse = 1.0 / (1.0 - g4 * g4)
    for d in (1, 3, 2):
        c_copies[d].wait_recv()
    own = cpart[0]
    x = (cgot[1] + g2 * (cgot[2] + g2 * (cgot[3] + g2 * own))) * inverse
    xown[...] = x
    x1 = own + g2 * x
    x2 = cgot[3] + g2 * x1
    x3 = cgot[2] + g2 * x2
    x_copies = {}
    for d, value in ((2, x2), (1, x1), (3, x3)):
        xsend[d] = value
        x_copies[d] = pltpu.make_async_remote_copy(
            xsend.at[d], xgot.at[d], xs.at[d], xr.at[d], device_id=chip_at(d), device_id_type=MESH
        )
        x_copies[d].start()

    f_copies = []
    for d in (0, 1, 3, 2):
        if d:
            x_copies[d].wait_recv()
        p = lax.rem(chip + 4 - d, 4)
        ps = pl.ds(p * PART, PART)
        even = xgot[d] if d else xown[...]
        odd = gain_of(p) * even + eo[0, ps]
        mine = jnp.where(core == 0, even, odd)
        other = jnp.where(core == 0, odd, even)
        cpart[4 + d] = other
        at = pl.ds(core * HALF + p * PART, PART)
        copy = pltpu.make_async_remote_copy(
            cpart.at[4 + d], out_ref.at[at], fs.at[d], fr.at[d], device_id=twin, device_id_type=MESH
        )
        copy.start()
        f_copies.append(copy)
        out_ref[at] = mine
    for copy in f_copies:
        copy.wait()

    for pair in halos:
        for copy in pair:
            copy.wait_send()
    for copy in n_copies:
        copy.wait_send()
    swap_copy.wait_send()
    for d in (1, 2, 3):
        c_copies[d].wait_send()
        x_copies[d].wait_send()


def by_vreg(x):
    split = x.reshape(x.shape[:-1] + (NV, 128))
    return jnp.swapaxes(split, -3, -2)


def body(n_space, start_states, coarse_gain, depth_level, depth_table, wet, block_count, neighbour, coriolis, tide):
    angles = np.arange(SLICES * STEPS) * (2.0 * math.pi / (SLICES * STEPS))
    trig = jnp.asarray(np.concatenate([np.cos(angles), np.sin(angles)]).astype(np.float32))
    f32, i32 = jnp.float32, jnp.int32
    field = pltpu.VMEM((NV, 8, 128), f32)
    field_i = pltpu.VMEM((NV, 8, 128), i32)
    state = pltpu.VMEM((3, NV, 8, 128), f32)
    edge = pltpu.VMEM((8, NV // 4, 8, 128), f32)
    rows = pltpu.VMEM((NV + 2, 8, 128), f32)
    vmem, anywhere, smem = (
        pl.BlockSpec(memory_space=pltpu.VMEM),
        pl.BlockSpec(memory_space=pl.ANY),
        pl.BlockSpec(memory_space=pltpu.SMEM),
    )
    dma = pltpu.SemaphoreType.DMA
    fields = [field] * 8 + [rows]
    out = pl.pallas_call(
        functools.partial(kernel, n_space),
        out_shape=jax.ShapeDtypeStruct((3 * NV, 8, 128), f32),
        in_specs=[anywhere] * 6 + [vmem, vmem, smem, smem],
        out_specs=vmem,
        scratch_shapes=[state, state, field_i, field_i, field, pltpu.VMEM((2, NV, 8, 128), f32), pltpu.VMEM((8, 128), f32)]
        + fields
        + fields
        + [edge] * 4
        + [pltpu.VMEM((3, 8, 128), i32)] * 4
        + [
            pltpu.VMEM((2, HALF, 8, 128), f32),
            pltpu.VMEM((HALF, 8, 128), f32),
            pltpu.VMEM((8, PART, 8, 128), f32),
            pltpu.VMEM((4, PART, 8, 128), f32),
            pltpu.VMEM((PART, 8, 128), f32),
            pltpu.VMEM((4, PART, 8, 128), f32),
            pltpu.VMEM((4, PART, 8, 128), f32),
            pltpu.VMEM((2, HALF, 8, 128), f32),
        ]
        + [dma((6,)), dma((8,)), dma((8,)), dma((8,)), dma((8,)), dma((4,)), dma((2,))]
        + [dma((4,))] * 6,
        compiler_params=pltpu.CompilerParams(
            collective_id=0, has_side_effects=True, vmem_limit_bytes=32 * 1024 * 1024
        ),
    )(
        by_vreg(start_states)[0],
        by_vreg(coarse_gain),
        by_vreg(depth_level),
        by_vreg(wet),
        by_vreg(coriolis),
        by_vreg(tide),
        depth_table.reshape(1, 64),
        neighbour,
        block_count,
        trig,
    )
    out = out.reshape(3, NV, 8, 128)
    return jnp.swapaxes(out, 1, 2).reshape(1, 3, 8, NV * 128)


def solution(mesh):
    return jax.shard_map(
        functools.partial(body, mesh.shape["space"]),
        mesh=mesh,
        in_specs=(
            P("tm", None, "space", None),
            P(None, "space", None),
            P("space", None),
            P(),
            P("space", None),
            P("space"),
            P("space", None),
            P("space", None),
            P(None, "space", None),
        ),
        out_specs=P("tm", None, "space", None),
        check_vma=False,
    )
```

```python
import functools
import math

import jax
import jax.numpy as jnp
from jax import lax
from jax.experimental import pallas as pl
from jax.experimental.pallas import tpu as pltpu
from jax.sharding import PartitionSpec as P

STEPS = 6
SLICES = 8
LEVELS = 64
NV = 32
FIXED = 5
CHUNK = 16
MESH = pl.DeviceIdType.MESH


def lanes():
    return lax.broadcasted_iota(jnp.int32, (8, 128), 1)


def turn(x, by):
    return pltpu.roll(x, by % 128, axis=x.ndim - 1)


def permuted(x, index, valid):
    if x.ndim == 2:
        picked = jnp.take_along_axis(x, index, axis=0, mode="promise_in_bounds")
        return jnp.where(valid, picked, 0.0)
    return jnp.stack([permuted(x[i], index, valid) for i in range(x.shape[0])])


def kernel(
    n_space,
    start_hbm, gain_hbm, level_hbm, wet_hbm, cor_hbm, tide_hbm, table_hbm, nb_hbm, count_hbm,
    out_ref,
    start, gain, lev, wet, cor, tide, table, nb, count, trig,
    depth_o, mask_o, t0_o, t1_o, c_o, eta_o, u_o, v_o, rf_o, re_o,
    depth_s, mask_s, t0_s, t1_s, c_s, eta_s, u_s, v_s, rf_s, re_s,
    pack_r, pack_l, got_r, got_l, nb_r, nb_l, nbgot_r, nbgot_l,
    eo, swap, cpart, cgot, xpart, xgot, final,
    load_sem, hs_r, hr_r, hs_l, hr_l, nsem, os, orr, ss, sr, cs, cr, xs, xr, fs, fr,
):
    m = lax.axis_index("tm")
    c = lax.axis_index("space")
    core = lax.rem(m, 2)
    chip = lax.div(m, 2)
    right = (m, lax.rem(c + 1, n_space))
    left = (m, lax.rem(c + n_space - 1, n_space))
    twin = (m + 1 - 2 * core, c)

    def chip_at(d):
        return (lax.rem(chip + d, 4) * 2 + core, c)

    barrier = pltpu.get_barrier_semaphore()
    peers = [right, left, twin, chip_at(1), chip_at(2), chip_at(3)]
    for peer in peers:
        pl.semaphore_signal(barrier, inc=1, device_id=peer, device_id_type=MESH)

    loads = []
    for j, (src, dst) in enumerate(
        [
            (wet_hbm, wet),
            (level_hbm, lev),
            (start_hbm, start),
            (cor_hbm, cor),
            (tide_hbm, tide),
            (gain_hbm, gain),
            (count_hbm, count),
            (nb_hbm, nb),
            (table_hbm, table),
        ]
    ):
        loads.append(pltpu.make_async_copy(src, dst, load_sem.at[j]))
    for j in (3, 6, 0, 4, 8, 1, 2, 7, 5):
        loads[j].start()

    lane = lanes()
    low = lane < 64
    col = lane & 63
    group = (lane >> 4) & 3
    near = col < 32

    slot = lax.broadcasted_iota(jnp.int32, (8, 128), 0)

    def packed(value, into, q0):
        for q in range(value.shape[0] // 4):
            to_r = to_l = value[4 * q]
            for i in range(1, 4):
                turned = turn(value[4 * q + i], 16 * i)
                to_r = jnp.where(group == (i + 3) % 4, turned, to_r)
                to_l = jnp.where(group == i, turned, to_l)
            pack_r[into, q0 + q] = to_r
            pack_l[into, q0 + q] = to_l

    def halo(j):
        at = pl.ds(4 * core, 4) if j < FIXED else pl.ds(0, 8)
        return (
            pltpu.make_async_remote_copy(
                pack_r.at[j, at], got_r.at[j, at], hs_r.at[j], hr_r.at[j], device_id=right, device_id_type=MESH
            ),
            pltpu.make_async_remote_copy(
                pack_l.at[j, at], got_l.at[j, at], hs_l.at[j], hr_l.at[j], device_id=left, device_id_type=MESH
            ),
        )

    def onward(j):
        at = pl.ds(4 * core, 4)
        return [
            pltpu.make_async_remote_copy(
                got.at[j, at], got.at[j, at], os.at[i, j], orr.at[i, j], device_id=twin, device_id_type=MESH
            )
            for i, got in enumerate((got_r, got_l))
        ]

    n_copies = (
        pltpu.make_async_remote_copy(nb_r, nbgot_r, nsem.at[0], nsem.at[1], device_id=right, device_id_type=MESH),
        pltpu.make_async_remote_copy(nb_l, nbgot_l, nsem.at[2], nsem.at[3], device_id=left, device_id_type=MESH),
    )
    halos = [halo(j) for j in range(8)]
    chunks = range(0, NV, CHUNK)

    def send(j):
        for copy in halos[j]:
            copy.start()

    def fixed(j, into, value_of):
        for half in (core, 1 - core):
            ks = pl.ds(half * CHUNK, CHUNK)
            value = value_of(ks)
            into[ks] = value
            if half is core:
                packed(value, j, 4 * core)
                if j == 0:
                    pl.semaphore_wait(barrier, len(peers))
                for copy in halos[j]:
                    copy.start()

    def depth_of(ks):
        index = lev[ks]
        return jnp.stack(
            [jnp.take_along_axis(entries, index[i], axis=1, mode="promise_in_bounds") for i in range(CHUNK)]
        )

    loads[3].wait()
    fixed(0, c_o, lambda ks: 0.3 * cor[ks])
    loads[6].wait()
    slot_live = slot < count[0]
    loads[0].wait()
    fixed(1, mask_o, lambda ks: jnp.where(jnp.logical_and(wet[ks] != 0, slot_live[None]), 0.15, 0.0))
    loads[4].wait()
    fixed(2, t0_o, lambda ks: (2.0 * mask_o[ks]) * tide[0, ks])
    fixed(3, t1_o, lambda ks: (2.0 * mask_o[ks]) * tide[1, ks])
    loads[1].wait()
    loads[8].wait()
    entries = jnp.full((8, 128), table[0])
    for n in range(1, LEVELS):
        entries = jnp.where(lane == n, table[n], entries)
    fixed(4, depth_o, depth_of)
    loads[2].wait()
    for j, (field, state) in enumerate(((1, u_o), (2, v_o), (0, eta_o))):
        for k0 in chunks:
            ks = pl.ds(k0, CHUNK)
            value = jnp.where(mask_o[ks] > 0.0, start[field, ks], 0.0)
            start[field, ks] = value
            state[ks] = value
            packed(value, FIXED + j, k0 // 4)
        for copy in halos[FIXED + j]:
            copy.start()
    loads[7].wait()
    def by_slot(side):
        entry = jnp.full((8, 128), nb[side, 0])
        for s in range(1, 8):
            entry = jnp.where(slot == s, nb[side, s], entry)
        return entry

    n_own, s_own, e_own, w_own = [by_slot(j) for j in range(4)]
    for j, (to_right, to_left) in enumerate([(n_own, n_own), (s_own, s_own), (e_own, w_own)]):
        nb_r[j] = to_right
        nb_l[j] = to_left
    for copy in n_copies:
        copy.start()
    for j in range(STEPS):
        for at, wave in ((0, math.cos), (STEPS, math.sin)):
            value = jnp.float32(0.0)
            for n in range(SLICES):
                value = jnp.where(m == n, jnp.float32(wave((n * STEPS + j) * (2.0 * math.pi / (SLICES * STEPS)))), value)
            trig[at + j] = value
    loads[5].wait()

    onwards = [onward(j) for j in range(FIXED)]
    for j in range(FIXED):
        for copy, further in zip(halos[j], onwards[j]):
            copy.wait_recv()
            further.start()
    for j, into in enumerate((c_s, mask_s, t0_s, t1_s, depth_s, u_s, v_s, eta_s)):
        for copy in onwards[j] if j < FIXED else halos[j]:
            copy.wait_recv()
        for q in range(NV // 4):
            from_l, from_r = got_r[j, q], got_l[j, q]
            for i in range(4):
                both = jnp.where(group == i, from_r, from_l)
                into[4 * q + i] = turn(both, 64 - 16 * i)

    for copy in n_copies:
        copy.wait_recv()
    n_r, s_r, w_r = nbgot_l[0], nbgot_l[1], nbgot_l[2]
    n_l, s_l, e_l = nbgot_r[0], nbgot_r[1], nbgot_r[2]

    def lookup(index):
        return jnp.maximum(index, 0), index >= 0

    x_own = lookup(jnp.where(near, e_own, w_own))
    y_own = lookup(jnp.where(low, s_own, n_own))
    x_strip = lookup(jnp.where(near, e_l, w_r))
    y_strip = lookup(jnp.where(low, jnp.where(near, n_r, n_l), jnp.where(near, s_r, s_l)))

    first = col == 0
    last = col == 63

    def slope_x(own, strip, both=True):
        strip_at = permuted(strip, *x_own)
        d_own = turn(jnp.where(first, strip_at, own), -1) - turn(jnp.where(last, strip_at, own), 1)
        if not both:
            return d_own, None
        own_at = permuted(own, *x_strip)
        d_strip = turn(jnp.where(first, own_at, strip), -1) - turn(jnp.where(last, own_at, strip), 1)
        return d_own, d_strip

    def slope_y(rows, k0, size, swapped):
        step = rows[pl.ds(k0 + 1, size + 1)] - rows[pl.ds(k0, size + 1)]
        here, after = step[:size], step[1:]
        return jnp.where(low, after, here) if swapped else jnp.where(low, here, after)

    def ends(rows, swapped):
        if swapped:
            edge = permuted(jnp.where(low, rows[1], rows[NV]), *y_strip)
        else:
            edge = permuted(jnp.where(low, rows[NV], rows[1]), *y_own)
        rows[0] = edge
        rows[NV + 1] = edge

    for k0 in chunks:
        ks, up = pl.ds(k0, CHUNK), pl.ds(k0 + 1, CHUNK)
        rf_o[up] = turn(depth_o[ks] * v_o[ks], 64)
        rf_s[up] = turn(depth_s[ks] * v_s[ks], 64)
    ends(rf_o, False)
    ends(rf_s, True)

    def surface(step, more):
        cosine, sine = trig[step], trig[STEPS + step]
        for k0 in chunks:
            ks, up = pl.ds(k0, CHUNK), pl.ds(k0 + 1, CHUNK)
            dx_o, dx_s = slope_x(depth_o[ks] * u_o[ks], depth_s[ks] * u_s[ks])
            for eta, mask, t0, t1, dx, dy, rows, turned in (
                (eta_o, mask_o, t0_o, t1_o, dx_o, slope_y(rf_o, k0, CHUNK, False), re_o, True),
                (eta_s, mask_s, t0_s, t1_s, dx_s, slope_y(rf_s, k0, CHUNK, True), re_s, more),
            ):
                value = eta[ks] + (t0[ks] * cosine + t1[ks] * sine) - mask[ks] * (dx + dy)
                eta[ks] = value
                if turned:
                    rows[up] = turn(value, 64)
        ends(re_o, False)
        if more:
            ends(re_s, True)

    def one_step(step, carry):
        surface(step, True)
        for k0 in chunks:
            ks, up = pl.ds(k0, CHUNK), pl.ds(k0 + 1, CHUNK)
            dx_o, dx_s = slope_x(eta_o[ks], eta_s[ks])
            for u_ref, v_ref, mask, cc, depth, dx, dy, rows in (
                (u_o, v_o, mask_o, c_o, depth_o, dx_o, slope_y(re_o, k0, CHUNK, False), rf_o),
                (u_s, v_s, mask_s, c_s, depth_s, dx_s, slope_y(re_s, k0, CHUNK, True), rf_s),
            ):
                u, v = u_ref[ks], v_ref[ks]
                u_ref[ks] = 0.985 * u + cc[ks] * v - mask[ks] * dx
                new_v = 0.985 * v - cc[ks] * u - mask[ks] * dy
                v_ref[ks] = new_v
                rows[up] = turn(depth[ks] * new_v, 64)
        ends(rf_o, False)
        ends(rf_s, True)
        return carry

    lax.fori_loop(0, STEPS - 1, one_step, 0)
    surface(STEPS - 1, False)

    def rows_of(half, s):
        return pl.ds(half * 16 + 8 * s, 8)

    def defect(half, s):
        k0 = half * 16 + 8 * s
        ks = pl.ds(k0, 8)
        dx, _ = slope_x(eta_o[ks], eta_s[ks], False)
        dy = slope_y(re_o, k0, 8, False)
        u, v = u_o[ks], v_o[ks]
        fine = (
            eta_o[ks],
            0.985 * u + c_o[ks] * v - mask_o[ks] * dx,
            0.985 * v - c_o[ks] * u - mask_o[ks] * dy,
        )
        return [fine[f] - gain[f, ks] * start[f, ks] for f in range(3)]

    swaps, c_copies, x_copies, f_copies = {}, {}, {}, []
    for s in range(2):
        for f, value in enumerate(defect(1 - core, s)):
            swap[s, f] = value
        swaps[s] = pltpu.make_async_remote_copy(
            swap.at[s], eo.at[core, s], ss.at[s], sr.at[s], device_id=twin, device_id_type=MESH
        )
        swaps[s].start()
    for s in range(2):
        for f, value in enumerate(defect(core, s)):
            eo[core, s, f] = value

    def quarter(d):
        return pl.ds(2 * lax.rem(chip + d, 4), 2)

    for s in range(2):
        swaps[s].wait_recv()
        cpart[s] = eo[1, s] + gain[:, rows_of(core, s)] * eo[0, s]
        for d in (2, 1, 3):
            c_copies[d, s] = pltpu.make_async_remote_copy(
                cpart.at[s, :, quarter(d)], cgot.at[d, s], cs.at[d, s], cr.at[d, s],
                device_id=chip_at(d), device_id_type=MESH,
            )
            c_copies[d, s].start()

    for s in range(2):
        g = gain[:, pl.ds(core * 16 + 8 * s + 2 * chip, 2)]
        g2 = g * g
        g4 = g2 * g2
        inverse = 1.0 / (1.0 - g4 * g4)
        for d in (1, 3, 2):
            c_copies[d, s].wait_recv()
        own = cpart[s, :, quarter(0)]
        x = (cgot[1, s] + g2 * (cgot[2, s] + g2 * (cgot[3, s] + g2 * own))) * inverse
        x1 = own + g2 * x
        x2 = cgot[3, s] + g2 * x1
        x3 = cgot[2, s] + g2 * x2
        for d, value in ((2, x2), (1, x1), (3, x3)):
            xpart[d, s] = value
            x_copies[d, s] = pltpu.make_async_remote_copy(
                xpart.at[d, s], xgot.at[s, :, quarter(0)], xs.at[d, s], xr.at[d, s],
                device_id=chip_at(d), device_id_type=MESH,
            )
            x_copies[d, s].start()
        xgot[s, :, quarter(0)] = x

    for s in range(2):
        for d in (1, 3, 2):
            x_copies[d, s].wait_recv()
        even = xgot[s]
        odd = gain[:, rows_of(core, s)] * even + eo[0, s]
        final[s] = jnp.where(core == 0, odd, even)
        at = rows_of(core, s)
        copy = pltpu.make_async_remote_copy(
            final.at[s], out_ref.at[:, at], fs.at[s], fr.at[s], device_id=twin, device_id_type=MESH
        )
        copy.start()
        f_copies.append(copy)
        out_ref[:, at] = jnp.where(core == 0, even, odd)
    for copy in f_copies:
        copy.wait()

    for pair in onwards:
        for copy in pair:
            copy.wait_send()
    for copies in (swaps, c_copies, x_copies):
        for copy in copies.values():
            copy.wait_send()
    for pair in halos:
        for copy in pair:
            copy.wait_send()
    for copy in n_copies:
        copy.wait_send()


def by_vreg(x):
    split = x.reshape(x.shape[:-1] + (NV, 128))
    return jnp.swapaxes(split, -3, -2)


def body(n_space, start_states, coarse_gain, depth_level, depth_table, wet, block_count, neighbour, coriolis, tide):
    f32, i32 = jnp.float32, jnp.int32
    field = pltpu.VMEM((NV, 8, 128), f32)
    field_i = pltpu.VMEM((NV, 8, 128), i32)
    state = pltpu.VMEM((3, NV, 8, 128), f32)
    edge = pltpu.VMEM((8, NV // 4, 8, 128), f32)
    rows = pltpu.VMEM((NV + 2, 8, 128), f32)
    vmem, hbm = (
        pl.BlockSpec(memory_space=pltpu.VMEM),
        pl.BlockSpec(memory_space=pltpu.HBM),
    )
    dma = pltpu.SemaphoreType.DMA
    fields = [field] * 8 + [rows] * 2
    out = pl.pallas_call(
        functools.partial(kernel, n_space),
        out_shape=pltpu.VMEM((3, NV, 8, 128), f32),
        in_specs=[hbm] * 9,
        out_specs=vmem,
        scratch_shapes=[state, state, field_i, field_i, field, pltpu.VMEM((2, NV, 8, 128), f32)]
        + [pltpu.SMEM((LEVELS,), f32), pltpu.SMEM((4, 8), i32), pltpu.SMEM((1,), i32), pltpu.SMEM((2 * STEPS,), f32)]
        + fields
        + fields
        + [edge] * 4
        + [pltpu.VMEM((3, 8, 128), i32)] * 4
        + [pltpu.VMEM((2, 2, 3, 8, 8, 128), f32)]
        + [pltpu.VMEM((2, 3, 8, 8, 128), f32)] * 2
        + [pltpu.VMEM((4, 2, 3, 2, 8, 128), f32)] * 2
        + [pltpu.VMEM((2, 3, 8, 8, 128), f32)] * 2
        + [dma((9,)), dma((8,)), dma((8,)), dma((8,)), dma((8,)), dma((4,)), dma((2, FIXED)), dma((2, FIXED))]
        + [dma((2,))] * 2
        + [dma((4, 2))] * 4
        + [dma((2,))] * 2,
        compiler_params=pltpu.CompilerParams(
            collective_id=0, has_side_effects=True, vmem_limit_bytes=int(60 * 1024 * 1024)
        ),
    )(
        by_vreg(start_states)[0],
        by_vreg(coarse_gain),
        by_vreg(depth_level),
        by_vreg(wet),
        by_vreg(coriolis),
        by_vreg(tide),
        depth_table,
        neighbour.T,
        block_count,
    )
    return jnp.swapaxes(out, 1, 2).reshape(1, 3, 8, NV * 128)


def solution(mesh):
    return jax.shard_map(
        functools.partial(body, mesh.shape["space"]),
        mesh=mesh,
        in_specs=(
            P("tm", None, "space", None),
            P(None, "space", None),
            P("space", None),
            P(),
            P("space", None),
            P("space"),
            P("space", None),
            P("space", None),
            P(None, "space", None),
        ),
        out_specs=P("tm", None, "space", None),
        check_vma=False,
    )
```

```python
import functools
import math

import jax
import jax.numpy as jnp
from jax import lax
from jax.experimental import pallas as pl
from jax.experimental.pallas import tpu as pltpu
from jax.sharding import PartitionSpec as P

STEPS = 6
SLICES = 8
LEVELS = 64
NV = 32
FIXED = 5
SUB = 2
CHUNK = 16
MESH = pl.DeviceIdType.MESH


def lanes():
    return lax.broadcasted_iota(jnp.int32, (8, 128), 1)


def turn(x, by):
    return pltpu.roll(x, by % 128, axis=x.ndim - 1)


def permuted(x, index, valid):
    if x.ndim == 2:
        picked = jnp.take_along_axis(x, index, axis=0, mode="promise_in_bounds")
        return jnp.where(valid, picked, 0.0)
    return jnp.stack([permuted(x[i], index, valid) for i in range(x.shape[0])])


def kernel(
    n_space,
    start_hbm, gain_hbm, level_hbm, wet_hbm, cor_hbm, tide_hbm, table_hbm, nb_hbm, count_hbm,
    out_ref,
    start, gain, lev, wet, cor, tide, table, nb, count, trig,
    depth_o, mask_o, t0_o, t1_o, c_o, u_o, v_o, eta_o, rf_o,
    depth_s, mask_s, t0_s, t1_s, c_s, u_s, v_s, eta_s, rf_s,
    pack_r, pack_l, got_r, got_l, nb_r, nb_l, nbgot_r, nbgot_l,
    first_state, factor, eo, swap, cpart, cgot, xpart, xgot, final,
    load_sem, hs_r, hr_r, hs_l, hr_l, nsem, os, orr, ss, sr, cs, cr, xs, xr, fs, fr,
):
    m = lax.axis_index("tm")
    c = lax.axis_index("space")
    core = lax.rem(m, 2)
    chip = lax.div(m, 2)
    right = (m, lax.rem(c + 1, n_space))
    left = (m, lax.rem(c + n_space - 1, n_space))
    twin = (m + 1 - 2 * core, c)

    def chip_at(d):
        return (lax.rem(chip + d, 4) * 2 + core, c)

    barrier = pltpu.get_barrier_semaphore()
    peers = [right, left, twin, chip_at(1), chip_at(2), chip_at(3)]
    for peer in peers:
        pl.semaphore_signal(barrier, inc=1, device_id=peer, device_id_type=MESH)

    loads = []
    for j, (src, dst) in enumerate(
        [
            (wet_hbm, wet),
            (level_hbm, lev),
            (start_hbm, start),
            (cor_hbm, cor),
            (tide_hbm, tide),
            (gain_hbm, gain),
            (count_hbm, count),
            (nb_hbm, nb),
            (table_hbm, table),
        ]
    ):
        loads.append(pltpu.make_async_copy(src, dst, load_sem.at[j]))
    for j in (3, 6, 0, 4, 8, 1, 2, 7, 5):
        loads[j].start()

    lane = lanes()
    low = lane < 64
    col = lane & 63
    group = (lane >> 4) & 3
    near = col < 32

    slot = lax.broadcasted_iota(jnp.int32, (8, 128), 0)

    def packed(value, into, q0):
        for q in range(value.shape[0] // 4):
            to_r = to_l = value[4 * q]
            for i in range(1, 4):
                turned = turn(value[4 * q + i], 16 * i)
                to_r = jnp.where(group == (i + 3) % 4, turned, to_r)
                to_l = jnp.where(group == i, turned, to_l)
            pack_r[into, q0 + q] = to_r
            pack_l[into, q0 + q] = to_l

    def halo(j):
        at = pl.ds(4 * core, 4) if j < FIXED else pl.ds(0, 8)
        return (
            pltpu.make_async_remote_copy(
                pack_r.at[j, at], got_r.at[j, at], hs_r.at[j], hr_r.at[j], device_id=right, device_id_type=MESH
            ),
            pltpu.make_async_remote_copy(
                pack_l.at[j, at], got_l.at[j, at], hs_l.at[j], hr_l.at[j], device_id=left, device_id_type=MESH
            ),
        )

    def onward(j):
        at = pl.ds(4 * core, 4)
        return [
            pltpu.make_async_remote_copy(
                got.at[j, at], got.at[j, at], os.at[i, j], orr.at[i, j], device_id=twin, device_id_type=MESH
            )
            for i, got in enumerate((got_r, got_l))
        ]

    n_copies = (
        pltpu.make_async_remote_copy(nb_r, nbgot_r, nsem.at[0], nsem.at[1], device_id=right, device_id_type=MESH),
        pltpu.make_async_remote_copy(nb_l, nbgot_l, nsem.at[2], nsem.at[3], device_id=left, device_id_type=MESH),
    )
    halos = [halo(j) for j in range(8)]
    chunks = range(0, NV, CHUNK)

    def send(j):
        for copy in halos[j]:
            copy.start()

    def split_rows(a, b):
        rows = []
        for j in range(a.shape[0]):
            rows += [jnp.where(low, a[j], turn(b[j], 64)), jnp.where(low, turn(a[j], 64), b[j])]
        return jnp.stack(rows)

    def fixed(j, into, value_of, masked=False):
        for half in (core, 1 - core):
            ks, at = pl.ds(half * CHUNK, CHUNK), pl.ds(half * 8, 8)
            value = split_rows(value_of(0, at), value_of(1, at))
            if masked:
                value = (2.0 * mask_o[ks]) * value
            into[ks] = value
            if half is core:
                packed(value, j, 4 * core)
                if j == 0:
                    pl.semaphore_wait(barrier, len(peers))
                for copy in halos[j]:
                    copy.start()

    def depth_of(i, at):
        index = lev[i, at]
        return jnp.stack(
            [jnp.take_along_axis(entries, index[n], axis=1, mode="promise_in_bounds") for n in range(8)]
        )

    loads[3].wait()
    fixed(0, c_o, lambda i, at: 0.3 * cor[i, at])
    loads[6].wait()
    slot_live = slot < count[0]
    loads[0].wait()
    fixed(1, mask_o, lambda i, at: jnp.where(jnp.logical_and(wet[i, at] != 0, slot_live[None]), 0.15, 0.0))
    loads[4].wait()
    fixed(2, t0_o, lambda i, at: tide[0, i, at], True)
    fixed(3, t1_o, lambda i, at: tide[1, i, at], True)
    loads[1].wait()
    loads[8].wait()
    entries = jnp.full((8, 128), table[0])
    for n in range(1, LEVELS):
        entries = jnp.where(lane == n, table[n], entries)
    fixed(4, depth_o, depth_of)
    loads[2].wait()
    for j, (field, state, skip) in enumerate(((1, u_o, 0), (2, v_o, 0), (0, eta_o, 1))):
        for k0 in chunks:
            ks, at = pl.ds(k0, CHUNK), pl.ds(k0 // 2, 8)
            value = jnp.where(mask_o[ks] > 0.0, split_rows(start[field, 0, at], start[field, 1, at]), 0.0)
            first_state[field, ks] = value
            state[pl.ds(k0 + skip, CHUNK)] = value
            packed(value, FIXED + j, k0 // 4)
        for copy in halos[FIXED + j]:
            copy.start()
    loads[7].wait()
    def by_slot(side):
        entry = jnp.full((8, 128), nb[side, 0])
        for s in range(1, 8):
            entry = jnp.where(slot == s, nb[side, s], entry)
        return entry

    n_own, s_own, e_own, w_own = [by_slot(j) for j in range(4)]
    for j, (to_right, to_left) in enumerate([(n_own, n_own), (s_own, s_own), (e_own, w_own)]):
        nb_r[j] = to_right
        nb_l[j] = to_left
    for copy in n_copies:
        copy.start()
    for j in range(STEPS):
        for at, wave in ((0, math.cos), (STEPS, math.sin)):
            value = jnp.float32(0.0)
            for n in range(SLICES):
                value = jnp.where(m == n, jnp.float32(wave((n * STEPS + j) * (2.0 * math.pi / (SLICES * STEPS)))), value)
            trig[at + j] = value
    loads[5].wait()
    for field in range(3):
        for k0 in chunks:
            at = pl.ds(k0 // 2, 8)
            factor[field, pl.ds(k0, CHUNK)] = split_rows(gain[field, 0, at], gain[field, 1, at])

    onwards = [onward(j) for j in range(FIXED)]
    for j in range(FIXED):
        for copy, further in zip(halos[j], onwards[j]):
            copy.wait_recv()
            further.start()
    for j, into in enumerate((c_s, mask_s, t0_s, t1_s, depth_s, u_s, v_s, eta_s)):
        for copy in onwards[j] if j < FIXED else halos[j]:
            copy.wait_recv()
        for q in range(NV // 4):
            from_l, from_r = got_r[j, q], got_l[j, q]
            for i in range(4):
                both = jnp.where(group == i, from_r, from_l)
                into[4 * q + i + (into is eta_s)] = turn(both, 64 - 16 * i)

    for copy in n_copies:
        copy.wait_recv()
    n_r, s_r, w_r = nbgot_l[0], nbgot_l[1], nbgot_l[2]
    n_l, s_l, e_l = nbgot_r[0], nbgot_r[1], nbgot_r[2]

    def lookup(index):
        return jnp.maximum(index, 0), index >= 0

    x_own = lookup(jnp.where(near, e_own, w_own))
    y_own = lookup(jnp.where(low, s_own, n_own))
    x_strip = lookup(jnp.where(near, e_l, w_r))
    y_strip = lookup(jnp.where(low, jnp.where(near, n_r, n_l), jnp.where(near, s_r, s_l)))

    first = col == 0
    last = col == 63

    def slope_x(own, strip, both=True):
        strip_at = permuted(strip, *x_own)
        d_own = turn(jnp.where(first, strip_at, own), -1) - turn(jnp.where(last, strip_at, own), 1)
        if not both:
            return d_own, None
        own_at = permuted(own, *x_strip)
        d_strip = turn(jnp.where(first, own_at, strip), -1) - turn(jnp.where(last, own_at, strip), 1)
        return d_own, d_strip

    def slope_y(rows, k0, size):
        return rows[pl.ds(k0 + 2, size)] - rows[pl.ds(k0, size)]

    def ends(rows, strip):
        above, below = turn(rows[1], 64), turn(rows[NV], 64)
        if strip:
            rows[NV + 1] = jnp.where(low, permuted(above, *y_strip), above)
            rows[0] = jnp.where(low, below, permuted(below, *y_strip))
        else:
            rows[NV + 1] = jnp.where(low, above, permuted(above, *y_own))
            rows[0] = jnp.where(low, permuted(below, *y_own), below)

    for k0 in chunks:
        ks, up = pl.ds(k0, CHUNK), pl.ds(k0 + 1, CHUNK)
        rf_o[up] = depth_o[ks] * v_o[ks]
        rf_s[up] = depth_s[ks] * v_s[ks]
    ends(rf_o, False)
    ends(rf_s, True)

    def surface(step, more):
        cosine, sine = trig[step], trig[STEPS + step]
        for k0 in range(0, NV, SUB):
            ks, up = pl.ds(k0, SUB), pl.ds(k0 + 1, SUB)
            dx_o, dx_s = slope_x(depth_o[ks] * u_o[ks], depth_s[ks] * u_s[ks])
            for eta, mask, t0, t1, dx, rows in (
                (eta_o, mask_o, t0_o, t1_o, dx_o, rf_o),
                (eta_s, mask_s, t0_s, t1_s, dx_s, rf_s),
            ):
                dy = slope_y(rows, k0, SUB)
                eta[up] = eta[up] + (t0[ks] * cosine + t1[ks] * sine) - mask[ks] * (dx + dy)
        ends(eta_o, False)
        if more:
            ends(eta_s, True)

    def one_step(step, carry):
        surface(step, True)
        for k0 in range(0, NV, SUB):
            ks, up = pl.ds(k0, SUB), pl.ds(k0 + 1, SUB)
            dx_o, dx_s = slope_x(eta_o[up], eta_s[up])
            for u_ref, v_ref, mask, cc, depth, dx, eta, rows in (
                (u_o, v_o, mask_o, c_o, depth_o, dx_o, eta_o, rf_o),
                (u_s, v_s, mask_s, c_s, depth_s, dx_s, eta_s, rf_s),
            ):
                dy = slope_y(eta, k0, SUB)
                u, v = u_ref[ks], v_ref[ks]
                u_ref[ks] = 0.985 * u + cc[ks] * v - mask[ks] * dx
                new_v = 0.985 * v - cc[ks] * u - mask[ks] * dy
                v_ref[ks] = new_v
                rows[up] = depth[ks] * new_v
        ends(rf_o, False)
        ends(rf_s, True)
        return carry

    lax.fori_loop(0, STEPS - 1, one_step, 0)
    surface(STEPS - 1, False)

    def rows_of(half, s):
        return pl.ds(half * 16 + 8 * s, 8)

    def defect(half, s):
        k0 = half * 16 + 8 * s
        ks, up = pl.ds(k0, 8), pl.ds(k0 + 1, 8)
        dx, _ = slope_x(eta_o[up], eta_s[up], False)
        dy = slope_y(eta_o, k0, 8)
        u, v = u_o[ks], v_o[ks]
        fine = (
            eta_o[up],
            0.985 * u + c_o[ks] * v - mask_o[ks] * dx,
            0.985 * v - c_o[ks] * u - mask_o[ks] * dy,
        )
        return [fine[f] - factor[f, ks] * first_state[f, ks] for f in range(3)]

    swaps, c_copies, x_copies, f_copies = {}, {}, {}, []
    for s in range(2):
        for f, value in enumerate(defect(1 - core, s)):
            swap[s, f] = value
        swaps[s] = pltpu.make_async_remote_copy(
            swap.at[s], eo.at[core, s], ss.at[s], sr.at[s], device_id=twin, device_id_type=MESH
        )
        swaps[s].start()
    for s in range(2):
        for f, value in enumerate(defect(core, s)):
            eo[core, s, f] = value

    def quarter(d):
        return pl.ds(2 * lax.rem(chip + d, 4), 2)

    for s in range(2):
        swaps[s].wait_recv()
        cpart[s] = eo[1, s] + factor[:, rows_of(core, s)] * eo[0, s]
        for d in (2, 1, 3):
            c_copies[d, s] = pltpu.make_async_remote_copy(
                cpart.at[s, :, quarter(d)], cgot.at[d, s], cs.at[d, s], cr.at[d, s],
                device_id=chip_at(d), device_id_type=MESH,
            )
            c_copies[d, s].start()

    for s in range(2):
        g = factor[:, pl.ds(core * 16 + 8 * s + 2 * chip, 2)]
        g2 = g * g
        g4 = g2 * g2
        inverse = 1.0 / (1.0 - g4 * g4)
        for d in (1, 3, 2):
            c_copies[d, s].wait_recv()
        own = cpart[s, :, quarter(0)]
        x = (cgot[1, s] + g2 * (cgot[2, s] + g2 * (cgot[3, s] + g2 * own))) * inverse
        x1 = own + g2 * x
        x2 = cgot[3, s] + g2 * x1
        x3 = cgot[2, s] + g2 * x2
        for d, value in ((2, x2), (1, x1), (3, x3)):
            xpart[d, s] = value
            x_copies[d, s] = pltpu.make_async_remote_copy(
                xpart.at[d, s], xgot.at[s, :, quarter(0)], xs.at[d, s], xr.at[d, s],
                device_id=chip_at(d), device_id_type=MESH,
            )
            x_copies[d, s].start()
        xgot[s, :, quarter(0)] = x

    def joined_rows(x):
        pairs = [(x[2 * j], x[2 * j + 1]) for j in range(x.shape[0] // 2)]
        return (
            jnp.stack([jnp.where(low, even, turn(odd, 64)) for even, odd in pairs]),
            jnp.stack([jnp.where(low, turn(even, 64), odd) for even, odd in pairs]),
        )

    for s in range(2):
        for d in (1, 3, 2):
            x_copies[d, s].wait_recv()
        even = xgot[s]
        odd = factor[:, rows_of(core, s)] * even + eo[0, s]
        other, mine = jnp.where(core == 0, odd, even), jnp.where(core == 0, even, odd)
        for f in range(3):
            for i, rows in enumerate(joined_rows(other[f])):
                final[s, f, i] = rows
        at = pl.ds(core * 8 + 4 * s, 4)
        copy = pltpu.make_async_remote_copy(
            final.at[s], out_ref.at[:, :, at], fs.at[s], fr.at[s], device_id=twin, device_id_type=MESH
        )
        copy.start()
        f_copies.append(copy)
        for f in range(3):
            for i, rows in enumerate(joined_rows(mine[f])):
                out_ref[f, i, at] = rows
    for copy in f_copies:
        copy.wait()

    for pair in onwards:
        for copy in pair:
            copy.wait_send()
    for copies in (swaps, c_copies, x_copies):
        for copy in copies.values():
            copy.wait_send()
    for pair in halos:
        for copy in pair:
            copy.wait_send()
    for copy in n_copies:
        copy.wait_send()


def by_vreg(x):
    split = x.reshape(x.shape[:-1] + (NV, 128))
    return jnp.swapaxes(split, -3, -2).reshape(x.shape[:-2] + (2, NV // 2, 8, 128))


def body(n_space, start_states, coarse_gain, depth_level, depth_table, wet, block_count, neighbour, coriolis, tide):
    f32, i32 = jnp.float32, jnp.int32
    field = pltpu.VMEM((NV, 8, 128), f32)
    state = pltpu.VMEM((3, NV, 8, 128), f32)
    whole = pltpu.VMEM((3, 2, NV // 2, 8, 128), f32)
    whole_i = pltpu.VMEM((2, NV // 2, 8, 128), i32)
    edge = pltpu.VMEM((8, NV // 4, 8, 128), f32)
    rows = pltpu.VMEM((NV + 2, 8, 128), f32)
    vmem, hbm = (
        pl.BlockSpec(memory_space=pltpu.VMEM),
        pl.BlockSpec(memory_space=pltpu.HBM),
    )
    dma = pltpu.SemaphoreType.DMA
    fields = [field] * 7 + [rows] * 2
    out = pl.pallas_call(
        functools.partial(kernel, n_space),
        out_shape=pltpu.VMEM((3, 2, NV // 2, 8, 128), f32),
        in_specs=[hbm] * 9,
        out_specs=vmem,
        scratch_shapes=[whole, whole, whole_i, whole_i]
        + [pltpu.VMEM((2, NV // 2, 8, 128), f32), pltpu.VMEM((2, 2, NV // 2, 8, 128), f32)]
        + [pltpu.SMEM((LEVELS,), f32), pltpu.SMEM((4, 8), i32), pltpu.SMEM((1,), i32), pltpu.SMEM((2 * STEPS,), f32)]
        + fields
        + fields
        + [edge] * 4
        + [pltpu.VMEM((3, 8, 128), i32)] * 4
        + [state, state]
        + [pltpu.VMEM((2, 2, 3, 8, 8, 128), f32)]
        + [pltpu.VMEM((2, 3, 8, 8, 128), f32)] * 2
        + [pltpu.VMEM((4, 2, 3, 2, 8, 128), f32)] * 2
        + [pltpu.VMEM((2, 3, 8, 8, 128), f32), pltpu.VMEM((2, 3, 2, 4, 8, 128), f32)]
        + [dma((9,)), dma((8,)), dma((8,)), dma((8,)), dma((8,)), dma((4,)), dma((2, FIXED)), dma((2, FIXED))]
        + [dma((2,))] * 2
        + [dma((4, 2))] * 4
        + [dma((2,))] * 2,
        compiler_params=pltpu.CompilerParams(
            collective_id=0, has_side_effects=True, vmem_limit_bytes=int(60 * 1024 * 1024)
        ),
    )(
        by_vreg(start_states)[0],
        by_vreg(coarse_gain),
        by_vreg(depth_level),
        by_vreg(wet),
        by_vreg(coriolis),
        by_vreg(tide),
        depth_table,
        neighbour.T,
        block_count,
    )
    return jnp.swapaxes(out.reshape(3, NV, 8, 128), 1, 2).reshape(1, 3, 8, NV * 128)


def solution(mesh):
    return jax.shard_map(
        functools.partial(body, mesh.shape["space"]),
        mesh=mesh,
        in_specs=(
            P("tm", None, "space", None),
            P(None, "space", None),
            P("space", None),
            P(),
            P("space", None),
            P("space"),
            P("space", None),
            P("space", None),
            P(None, "space", None),
        ),
        out_specs=P("tm", None, "space", None),
        check_vma=False,
    )
```

```python
import functools
import math

import jax
import jax.numpy as jnp
from jax import lax
from jax.experimental import pallas as pl
from jax.experimental.pallas import tpu as pltpu
from jax.sharding import PartitionSpec as P

STEPS = 6
SLICES = 8
LEVELS = 64
NV = 32
FIXED = 5
SUB = 2
CHUNK = 16
MESH = pl.DeviceIdType.MESH


def lanes():
    return lax.broadcasted_iota(jnp.int32, (8, 128), 1)


def turn(x, by):
    return pltpu.roll(x, by % 128, axis=x.ndim - 1)


def permuted(x, index, valid):
    if x.ndim == 2:
        picked = jnp.take_along_axis(x, index, axis=0, mode="promise_in_bounds")
        return jnp.where(valid, picked, 0.0)
    return jnp.stack([permuted(x[i], index, valid) for i in range(x.shape[0])])


def kernel(
    n_space,
    start_hbm, gain_hbm, level_hbm, wet_hbm, cor_hbm, tide_hbm, table_hbm, nb_hbm, count_hbm,
    out_ref,
    start, gain, lev, wet, cor, tide, table, nb, count, trig,
    depth_o, mask_o, t0_o, t1_o, c_o, u_o, v_o, eta_o, rf_o,
    depth_s, mask_s, t0_s, t1_s, c_s, u_s, v_s, eta_s, rf_s,
    pack_r, pack_l, got_r, got_l, nb_r, nb_l, nbgot_r, nbgot_l,
    first_state, factor, eo, swap, cpart, cgot, xpart, xgot, final,
    load_sem, hs_r, hr_r, hs_l, hr_l, nsem, os, orr, ss, sr, cs, cr, xs, xr, fs, fr,
):
    m = lax.axis_index("tm")
    c = lax.axis_index("space")
    core = lax.rem(m, 2)
    chip = lax.div(m, 2)
    right = (m, lax.rem(c + 1, n_space))
    left = (m, lax.rem(c + n_space - 1, n_space))
    twin = (m + 1 - 2 * core, c)

    def chip_at(d):
        return (lax.rem(chip + d, 4) * 2 + core, c)

    barrier = pltpu.get_barrier_semaphore()
    peers = [right, left, twin, chip_at(1), chip_at(2), chip_at(3)]
    for peer in peers:
        pl.semaphore_signal(barrier, inc=1, device_id=peer, device_id_type=MESH)

    loads = []
    for j, (src, dst) in enumerate(
        [
            (wet_hbm, wet),
            (level_hbm, lev),
            (start_hbm, start),
            (cor_hbm, cor),
            (tide_hbm, tide),
            (gain_hbm, gain),
            (count_hbm, count),
            (nb_hbm, nb),
            (table_hbm, table),
        ]
    ):
        loads.append(pltpu.make_async_copy(src, dst, load_sem.at[j]))
    for j in (3, 7, 6, 0, 4, 8, 1, 2, 5):
        loads[j].start()

    lane = lanes()
    low = lane < 64
    col = lane & 63
    group = (lane >> 4) & 3
    near = col < 32

    slot = lax.broadcasted_iota(jnp.int32, (8, 128), 0)

    def packed(value, into, q0):
        for q in range(value.shape[0] // 4):
            to_r = to_l = value[4 * q]
            for i in range(1, 4):
                turned = turn(value[4 * q + i], 16 * i)
                to_r = jnp.where(group == (i + 3) % 4, turned, to_r)
                to_l = jnp.where(group == i, turned, to_l)
            pack_r[into, q0 + q] = to_r
            pack_l[into, q0 + q] = to_l

    def halo(j):
        at = pl.ds(4 * core, 4) if j < FIXED else pl.ds(0, 8)
        return (
            pltpu.make_async_remote_copy(
                pack_r.at[j, at], got_r.at[j, at], hs_r.at[j], hr_r.at[j], device_id=right, device_id_type=MESH
            ),
            pltpu.make_async_remote_copy(
                pack_l.at[j, at], got_l.at[j, at], hs_l.at[j], hr_l.at[j], device_id=left, device_id_type=MESH
            ),
        )

    def onward(j):
        at = pl.ds(4 * core, 4)
        return [
            pltpu.make_async_remote_copy(
                got.at[j, at], got.at[j, at], os.at[i, j], orr.at[i, j], device_id=twin, device_id_type=MESH
            )
            for i, got in enumerate((got_r, got_l))
        ]

    n_copies = (
        pltpu.make_async_remote_copy(nb_r, nbgot_r, nsem.at[0], nsem.at[1], device_id=right, device_id_type=MESH),
        pltpu.make_async_remote_copy(nb_l, nbgot_l, nsem.at[2], nsem.at[3], device_id=left, device_id_type=MESH),
    )
    halos = [halo(j) for j in range(8)]
    chunks = range(0, NV, CHUNK)

    def send(j):
        for copy in halos[j]:
            copy.start()

    def split_rows(a, b):
        rows = []
        for j in range(a.shape[0]):
            rows += [jnp.where(low, a[j], turn(b[j], 64)), jnp.where(low, turn(a[j], 64), b[j])]
        return jnp.stack(rows)

    def fixed(j, into, value_of, masked=False):
        for half in (core, 1 - core):
            ks, at = pl.ds(half * CHUNK, CHUNK), pl.ds(half * 8, 8)
            value = split_rows(value_of(0, at), value_of(1, at))
            if masked:
                value = (2.0 * mask_o[ks]) * value
            into[ks] = value
            if half is core:
                packed(value, j, 4 * core)
                if j == 0:
                    pl.semaphore_wait(barrier, len(peers))
                for copy in halos[j]:
                    copy.start()

    def depth_of(i, at):
        index = lev[i, at]
        return jnp.stack(
            [jnp.take_along_axis(entries, index[n], axis=1, mode="promise_in_bounds") for n in range(8)]
        )

    loads[3].wait()
    fixed(0, c_o, lambda i, at: 0.3 * cor[i, at])
    loads[7].wait()
    def by_slot(side):
        entry = jnp.full((8, 128), nb[side, 0])
        for s in range(1, 8):
            entry = jnp.where(slot == s, nb[side, s], entry)
        return entry

    n_own, s_own, e_own, w_own = [by_slot(j) for j in range(4)]
    for j, (to_right, to_left) in enumerate([(n_own, n_own), (s_own, s_own), (e_own, w_own)]):
        nb_r[j] = to_right
        nb_l[j] = to_left
    for copy in n_copies:
        copy.start()
    loads[6].wait()
    slot_live = slot < count[0]
    loads[0].wait()
    fixed(1, mask_o, lambda i, at: jnp.where(jnp.logical_and(wet[i, at] != 0, slot_live[None]), 0.15, 0.0))
    loads[4].wait()
    fixed(2, t0_o, lambda i, at: tide[0, i, at], True)
    fixed(3, t1_o, lambda i, at: tide[1, i, at], True)
    loads[1].wait()
    loads[8].wait()
    entries = jnp.full((8, 128), table[0])
    for n in range(1, LEVELS):
        entries = jnp.where(lane == n, table[n], entries)
    fixed(4, depth_o, depth_of)
    loads[2].wait()
    for j, (field, state, skip) in enumerate(((1, u_o, 0), (2, v_o, 0), (0, eta_o, 1))):
        for k0 in chunks:
            ks, at = pl.ds(k0, CHUNK), pl.ds(k0 // 2, 8)
            value = jnp.where(mask_o[ks] > 0.0, split_rows(start[field, 0, at], start[field, 1, at]), 0.0)
            first_state[field, ks] = value
            state[pl.ds(k0 + skip, CHUNK)] = value
            packed(value, FIXED + j, k0 // 4)
        for copy in halos[FIXED + j]:
            copy.start()
    for j in range(STEPS):
        for at, wave in ((0, math.cos), (STEPS, math.sin)):
            value = jnp.float32(0.0)
            for n in range(SLICES):
                value = jnp.where(m == n, jnp.float32(wave((n * STEPS + j) * (2.0 * math.pi / (SLICES * STEPS)))), value)
            trig[at + j] = value
    loads[5].wait()
    for field in range(3):
        for k0 in chunks:
            at = pl.ds(k0 // 2, 8)
            factor[field, pl.ds(k0, CHUNK)] = split_rows(gain[field, 0, at], gain[field, 1, at])

    onwards = [onward(j) for j in range(FIXED)]
    for j in range(FIXED):
        for copy, further in zip(halos[j], onwards[j]):
            copy.wait_recv()
            further.start()
    for j, into in enumerate((c_s, mask_s, t0_s, t1_s, depth_s, u_s, v_s, eta_s)):
        for copy in onwards[j] if j < FIXED else halos[j]:
            copy.wait_recv()
        for q in range(NV // 4):
            from_l, from_r = got_r[j, q], got_l[j, q]
            for i in range(4):
                both = jnp.where(group == i, from_r, from_l)
                into[4 * q + i + (into is eta_s)] = turn(both, 64 - 16 * i)

    for copy in n_copies:
        copy.wait_recv()
    n_r, s_r, w_r = nbgot_l[0], nbgot_l[1], nbgot_l[2]
    n_l, s_l, e_l = nbgot_r[0], nbgot_r[1], nbgot_r[2]

    def lookup(index):
        return jnp.maximum(index, 0), index >= 0

    x_own = lookup(jnp.where(near, e_own, w_own))
    y_own = lookup(jnp.where(low, s_own, n_own))
    x_strip = lookup(jnp.where(near, e_l, w_r))
    y_strip = lookup(jnp.where(low, jnp.where(near, n_r, n_l), jnp.where(near, s_r, s_l)))

    first = col == 0
    last = col == 63

    def slope_x(own, strip, both=True):
        strip_at = permuted(strip, *x_own)
        d_own = turn(jnp.where(first, strip_at, own), -1) - turn(jnp.where(last, strip_at, own), 1)
        if not both:
            return d_own, None
        own_at = permuted(own, *x_strip)
        d_strip = turn(jnp.where(first, own_at, strip), -1) - turn(jnp.where(last, own_at, strip), 1)
        return d_own, d_strip

    def slope_y(rows, k0, size):
        return rows[pl.ds(k0 + 2, size)] - rows[pl.ds(k0, size)]

    def ends(rows, strip):
        above, below = turn(rows[1], 64), turn(rows[NV], 64)
        if strip:
            rows[NV + 1] = jnp.where(low, permuted(above, *y_strip), above)
            rows[0] = jnp.where(low, below, permuted(below, *y_strip))
        else:
            rows[NV + 1] = jnp.where(low, above, permuted(above, *y_own))
            rows[0] = jnp.where(low, permuted(below, *y_own), below)

    for k0 in chunks:
        ks, up = pl.ds(k0, CHUNK), pl.ds(k0 + 1, CHUNK)
        rf_o[up] = depth_o[ks] * v_o[ks]
        rf_s[up] = depth_s[ks] * v_s[ks]
    ends(rf_o, False)
    ends(rf_s, True)

    def surface(step, more):
        cosine, sine = trig[step], trig[STEPS + step]
        for k0 in range(0, NV, SUB):
            ks, up = pl.ds(k0, SUB), pl.ds(k0 + 1, SUB)
            dx_o, dx_s = slope_x(depth_o[ks] * u_o[ks], depth_s[ks] * u_s[ks])
            for eta, mask, t0, t1, dx, rows in (
                (eta_o, mask_o, t0_o, t1_o, dx_o, rf_o),
                (eta_s, mask_s, t0_s, t1_s, dx_s, rf_s),
            ):
                dy = slope_y(rows, k0, SUB)
                eta[up] = eta[up] + (t0[ks] * cosine + t1[ks] * sine) - mask[ks] * (dx + dy)
        ends(eta_o, False)
        if more:
            ends(eta_s, True)

    def one_step(step, carry):
        surface(step, True)
        for k0 in range(0, NV, SUB):
            ks, up = pl.ds(k0, SUB), pl.ds(k0 + 1, SUB)
            dx_o, dx_s = slope_x(eta_o[up], eta_s[up])
            for u_ref, v_ref, mask, cc, depth, dx, eta, rows in (
                (u_o, v_o, mask_o, c_o, depth_o, dx_o, eta_o, rf_o),
                (u_s, v_s, mask_s, c_s, depth_s, dx_s, eta_s, rf_s),
            ):
                dy = slope_y(eta, k0, SUB)
                u, v = u_ref[ks], v_ref[ks]
                u_ref[ks] = 0.985 * u + cc[ks] * v - mask[ks] * dx
                new_v = 0.985 * v - cc[ks] * u - mask[ks] * dy
                v_ref[ks] = new_v
                rows[up] = depth[ks] * new_v
        ends(rf_o, False)
        ends(rf_s, True)
        return carry

    lax.fori_loop(0, STEPS - 1, one_step, 0)
    surface(STEPS - 1, False)

    def rows_of(half, s):
        return pl.ds(half * 16 + 8 * s, 8)

    def defect(half, s):
        k0 = half * 16 + 8 * s
        ks, up = pl.ds(k0, 8), pl.ds(k0 + 1, 8)
        dx, _ = slope_x(eta_o[up], eta_s[up], False)
        dy = slope_y(eta_o, k0, 8)
        u, v = u_o[ks], v_o[ks]
        fine = (
            eta_o[up],
            0.985 * u + c_o[ks] * v - mask_o[ks] * dx,
            0.985 * v - c_o[ks] * u - mask_o[ks] * dy,
        )
        return [fine[f] - factor[f, ks] * first_state[f, ks] for f in range(3)]

    swaps, c_copies, x_copies, f_copies = {}, {}, {}, []
    for s in range(2):
        for f, value in enumerate(defect(1 - core, s)):
            swap[s, f] = value
        swaps[s] = pltpu.make_async_remote_copy(
            swap.at[s], eo.at[core, s], ss.at[s], sr.at[s], device_id=twin, device_id_type=MESH
        )
        swaps[s].start()
    for s in range(2):
        for f, value in enumerate(defect(core, s)):
            eo[core, s, f] = value

    def quarter(d):
        return pl.ds(2 * lax.rem(chip + d, 4), 2)

    for s in range(2):
        swaps[s].wait_recv()
        cpart[s] = eo[1, s] + factor[:, rows_of(core, s)] * eo[0, s]
        for d in (2, 1, 3):
            c_copies[d, s] = pltpu.make_async_remote_copy(
                cpart.at[s, :, quarter(d)], cgot.at[d, s], cs.at[d, s], cr.at[d, s],
                device_id=chip_at(d), device_id_type=MESH,
            )
            c_copies[d, s].start()

    for s in range(2):
        g = factor[:, pl.ds(core * 16 + 8 * s + 2 * chip, 2)]
        g2 = g * g
        g4 = g2 * g2
        inverse = 1.0 / (1.0 - g4 * g4)
        for d in (1, 3, 2):
            c_copies[d, s].wait_recv()
        own = cpart[s, :, quarter(0)]
        x = (cgot[1, s] + g2 * (cgot[2, s] + g2 * (cgot[3, s] + g2 * own))) * inverse
        x1 = own + g2 * x
        x2 = cgot[3, s] + g2 * x1
        x3 = cgot[2, s] + g2 * x2
        for d, value in ((2, x2), (1, x1), (3, x3)):
            xpart[d, s] = value
            x_copies[d, s] = pltpu.make_async_remote_copy(
                xpart.at[d, s], xgot.at[s, :, quarter(0)], xs.at[d, s], xr.at[d, s],
                device_id=chip_at(d), device_id_type=MESH,
            )
            x_copies[d, s].start()
        xgot[s, :, quarter(0)] = x

    def joined_rows(x):
        pairs = [(x[2 * j], x[2 * j + 1]) for j in range(x.shape[0] // 2)]
        return (
            jnp.stack([jnp.where(low, even, turn(odd, 64)) for even, odd in pairs]),
            jnp.stack([jnp.where(low, turn(even, 64), odd) for even, odd in pairs]),
        )

    for s in range(2):
        for d in (1, 3, 2):
            x_copies[d, s].wait_recv()
        even = xgot[s]
        odd = factor[:, rows_of(core, s)] * even + eo[0, s]
        other, mine = jnp.where(core == 0, odd, even), jnp.where(core == 0, even, odd)
        for f in range(3):
            for i, rows in enumerate(joined_rows(other[f])):
                final[s, f, i] = rows
        at = pl.ds(core * 8 + 4 * s, 4)
        copy = pltpu.make_async_remote_copy(
            final.at[s], out_ref.at[:, :, at], fs.at[s], fr.at[s], device_id=twin, device_id_type=MESH
        )
        copy.start()
        f_copies.append(copy)
        for f in range(3):
            for i, rows in enumerate(joined_rows(mine[f])):
                out_ref[f, i, at] = rows
    for copy in f_copies:
        copy.wait()

    for pair in onwards:
        for copy in pair:
            copy.wait_send()
    for copies in (swaps, c_copies, x_copies):
        for copy in copies.values():
            copy.wait_send()
    for pair in halos:
        for copy in pair:
            copy.wait_send()
    for copy in n_copies:
        copy.wait_send()


def by_vreg(x):
    split = x.reshape(x.shape[:-1] + (NV, 128))
    return jnp.swapaxes(split, -3, -2).reshape(x.shape[:-2] + (2, NV // 2, 8, 128))


def body(n_space, start_states, coarse_gain, depth_level, depth_table, wet, block_count, neighbour, coriolis, tide):
    f32, i32 = jnp.float32, jnp.int32
    field = pltpu.VMEM((NV, 8, 128), f32)
    state = pltpu.VMEM((3, NV, 8, 128), f32)
    whole = pltpu.VMEM((3, 2, NV // 2, 8, 128), f32)
    whole_i = pltpu.VMEM((2, NV // 2, 8, 128), i32)
    edge = pltpu.VMEM((8, NV // 4, 8, 128), f32)
    rows = pltpu.VMEM((NV + 2, 8, 128), f32)
    vmem, hbm = (
        pl.BlockSpec(memory_space=pltpu.VMEM),
        pl.BlockSpec(memory_space=pltpu.HBM),
    )
    dma = pltpu.SemaphoreType.DMA
    fields = [field] * 7 + [rows] * 2
    out = pl.pallas_call(
        functools.partial(kernel, n_space),
        out_shape=pltpu.VMEM((3, 2, NV // 2, 8, 128), f32),
        in_specs=[hbm] * 9,
        out_specs=vmem,
        scratch_shapes=[whole, whole, whole_i, whole_i]
        + [pltpu.VMEM((2, NV // 2, 8, 128), f32), pltpu.VMEM((2, 2, NV // 2, 8, 128), f32)]
        + [pltpu.SMEM((LEVELS,), f32), pltpu.SMEM((4, 8), i32), pltpu.SMEM((1,), i32), pltpu.SMEM((2 * STEPS,), f32)]
        + fields
        + fields
        + [edge] * 4
        + [pltpu.VMEM((3, 8, 128), i32)] * 4
        + [state, state]
        + [pltpu.VMEM((2, 2, 3, 8, 8, 128), f32)]
        + [pltpu.VMEM((2, 3, 8, 8, 128), f32)] * 2
        + [pltpu.VMEM((4, 2, 3, 2, 8, 128), f32)] * 2
        + [pltpu.VMEM((2, 3, 8, 8, 128), f32), pltpu.VMEM((2, 3, 2, 4, 8, 128), f32)]
        + [dma((9,)), dma((8,)), dma((8,)), dma((8,)), dma((8,)), dma((4,)), dma((2, FIXED)), dma((2, FIXED))]
        + [dma((2,))] * 2
        + [dma((4, 2))] * 4
        + [dma((2,))] * 2,
        compiler_params=pltpu.CompilerParams(
            collective_id=0, has_side_effects=True, vmem_limit_bytes=int(60 * 1024 * 1024)
        ),
    )(
        by_vreg(start_states)[0],
        by_vreg(coarse_gain),
        by_vreg(depth_level),
        by_vreg(wet),
        by_vreg(coriolis),
        by_vreg(tide),
        depth_table,
        neighbour.T,
        block_count,
    )
    return jnp.swapaxes(out.reshape(3, NV, 8, 128), 1, 2).reshape(1, 3, 8, NV * 128)


def solution(mesh):
    return jax.shard_map(
        functools.partial(body, mesh.shape["space"]),
        mesh=mesh,
        in_specs=(
            P("tm", None, "space", None),
            P(None, "space", None),
            P("space", None),
            P(),
            P("space", None),
            P("space"),
            P("space", None),
            P("space", None),
            P(None, "space", None),
        ),
        out_specs=P("tm", None, "space", None),
        check_vma=False,
    )
```
